512 devices in a mesh: seq: 64 (over y, x, core), head: 8 (over z).
Axes of the slice: x: 4, y: 8, z: 8, core: 2. Of those that a mesh axis runs over, the one named last changes fastest.
Arguments:
- queries: bfloat16 [2, 16384, 4096], P(None, ('seq', 'head')), may hold values from -6 to 6
- keys: bfloat16 [2, 16384, 4096], P(None, ('seq', 'head')), may hold values from -6 to 6
- values: bfloat16 [2, 16384, 4096], P(None, ('seq', 'head')), may hold values from -6 to 6
- rates: bfloat16 [2, 16384, 8], P(None, ('seq', 'head')), may hold values from 0.049804688 to 1
- fast_init: float32 [8, 3, 512, 256], P('head', None, 'seq'), may hold values from -0.25 to 0.25
Outputs:
- outputs: bfloat16 [2, 16384, 4096], P(None, 'seq', 'head')
The draws below stay inside these ranges and needn't reach their ends.
All inputs are finite; a program needn't handle non-finite values.
Results may differ from the reference program's by a relative error of at most 0.0085.
Values may be sent and summed in bfloat16 or wider, within the bound.
A program may use at most 64 MiB of HBM per device.

```python
import math
import jax
import jax.numpy as jnp
from jax import lax

HEADS = 8
HD = 512
FH = 256
BLOCK_COUNT = 2
BLOCK_TOKENS = 16384
D = 4096


def shard_levels(key, dims, split, least, largest):
    level = 1.0
    for axis_at, blocks in split:
        draws = jax.random.uniform(jax.random.fold_in(jax.random.fold_in(key, 6), axis_at), (blocks,), jnp.float32, least / len(split), largest / len(split))
        level = level * jnp.repeat(jnp.exp(draws), dims[axis_at] // blocks).reshape((-1,) + (1,) * (len(dims) - 1 - axis_at))
    return level


def noise(key, shape, deviation, most, pieces=(), kind=jnp.bfloat16):
    values = deviation * jax.random.normal(key, shape, jnp.float32)
    if pieces:
        values = values * shard_levels(key, shape, pieces, -0.22, 0.18)
    return jnp.clip(values, -most, most).astype(kind)


def setup_inputs(seed: int = 0) -> dict:
    key_list = jax.random.split(jax.random.key(seed), 6)
    queries = noise(key_list[0], (BLOCK_COUNT, BLOCK_TOKENS, D), 1.0, 6.0, ((1, 512),))
    keys = noise(key_list[1], (BLOCK_COUNT, BLOCK_TOKENS, D), 1.0, 6.0, ((1, 512),))
    values = noise(key_list[2], (BLOCK_COUNT, BLOCK_TOKENS, D), 1.0, 6.0, ((1, 512),))
    rates = jnp.clip(jnp.exp(math.log(1.0) - 2.9996462 * jax.random.uniform(key_list[3], (BLOCK_COUNT, BLOCK_TOKENS, HEADS), jnp.float32) ** shard_levels(key_list[3], (BLOCK_COUNT, BLOCK_TOKENS, HEADS), ((1, 512),), -0.2, 0.2)), 0.049804688, 1.0).astype(jnp.bfloat16)
    fast_init = noise(key_list[4], (HEADS, 3, HD, FH), HD ** -0.5, 0.25, ((0, 8), (2, 64)), jnp.float32)
    return {"queries": queries, "keys": keys, "values": values, "rates": rates, "fast_init": fast_init}


EPSILON = 1e-06
COEF_A = 3.4445
COEF_B = -4.775
COEF_C = 2.0315
LEARNING_STEP = 0.5
FULL_PRECISION = lax.Precision.HIGHEST

def silu_parts(gate_pre):
    sigmoid_value = jax.nn.sigmoid(gate_pre)
    return (gate_pre * sigmoid_value, sigmoid_value * (1.0 + gate_pre * (1.0 - sigmoid_value)))

def contract_rows(left, right):
    return lax.dot_general(left, right, (((0,), (0,)), ((), ())), preferred_element_type=jnp.float32)

def gram_of(weight_matrices):
    return jnp.einsum('qha,qhk->qak', weight_matrices, weight_matrices, precision=FULL_PRECISION)

def newton_schulz(gradients):
    gram_matrix = gram_of(gradients)
    norm_value = jnp.sqrt(jnp.trace(gram_matrix, axis1=1, axis2=2)) + EPSILON
    current_weights = gradients / norm_value[:, None, None]
    gram_matrix = gram_matrix / (norm_value * norm_value)[:, None, None]
    identity = jnp.eye(gram_matrix.shape[-1], dtype=gram_matrix.dtype)
    for sweeps in range(2):
        if sweeps > 0:
            gram_matrix = gram_of(current_weights)
        square = jnp.einsum('mfg,mgk->mfk', gram_matrix, gram_matrix, precision=FULL_PRECISION)
        polynomial_update = COEF_A * identity + COEF_B * gram_matrix + COEF_C * square
        current_weights = jnp.einsum('tid,tdp->tip', current_weights, polynomial_update, precision=FULL_PRECISION)
    return current_weights

def group_step(weights, query_rows, key_rows, value_rows, rate_rows):
    low = weights.astype(jnp.bfloat16)
    gate_pre = jnp.dot(key_rows, low[0], preferred_element_type=jnp.float32)
    up_proj = jnp.dot(key_rows, low[1], preferred_element_type=jnp.float32)
    activated_hidden, slope_value = silu_parts(gate_pre)
    hidden = (activated_hidden * up_proj).astype(jnp.bfloat16)
    out_grad = (-(rate_rows.astype(jnp.float32)[:, None] * value_rows.astype(jnp.float32))).astype(jnp.bfloat16)
    hidden_grad = jnp.dot(out_grad, low[2], preferred_element_type=jnp.float32)
    gate_grad = (hidden_grad * up_proj * slope_value).astype(jnp.bfloat16)
    up_grad = (hidden_grad * activated_hidden).astype(jnp.bfloat16)
    gradients = jnp.stack([contract_rows(key_rows, gate_grad), contract_rows(key_rows, up_grad), contract_rows(out_grad, hidden)])
    weights = weights - LEARNING_STEP * newton_schulz(gradients)
    low = weights.astype(jnp.bfloat16)
    query_gate = jnp.dot(query_rows, low[0], preferred_element_type=jnp.float32)
    query_up = jnp.dot(query_rows, low[1], preferred_element_type=jnp.float32)
    query_act, unused_slope = silu_parts(query_gate)
    query_hidden = (query_act * query_up).astype(jnp.bfloat16)
    result = lax.dot_general(query_hidden, low[2], (((1,), (1,)), ((), ())), preferred_element_type=jnp.float32)
    return (weights, result.astype(jnp.bfloat16))

def reference(queries, keys, values, rates, fast_init):

    def head_pass(head_index):
        start = (head_index * HD).astype(jnp.int32)
        query_head = lax.dynamic_slice_in_dim(queries, start, HD, 2)
        key_head = lax.dynamic_slice_in_dim(keys, start, HD, 2)
        value_head = lax.dynamic_slice_in_dim(values, start, HD, 2)
        rate_head = lax.dynamic_slice_in_dim(rates, head_index.astype(jnp.int32), 1, 2)[:, :, 0]
        weights = fast_init[head_index]
        results = []
        for group_index in range(BLOCK_COUNT):
            weights, result = group_step(weights, query_head[group_index], key_head[group_index], value_head[group_index], rate_head[group_index])
            results.append(result)
        return jnp.stack(results)
    stacked = lax.map(head_pass, jnp.arange(HEADS, dtype=jnp.int32))
    return jnp.transpose(stacked, (1, 2, 0, 3)).reshape(BLOCK_COUNT, BLOCK_TOKENS, HEADS * HD)
```

```python
import jax
import jax.numpy as jnp
from jax import lax
from jax.experimental import pallas as pl
from jax.experimental.pallas import tpu as pltpu
from jax.sharding import Mesh
from jax.sharding import PartitionSpec as P

EPSILON = 1e-06
COEF_A = 3.4445
COEF_B = -4.775
COEF_C = 2.0315
LEARNING_STEP = 0.5
MESH = pl.DeviceIdType.MESH
BF16 = jnp.bfloat16
F32 = jnp.float32


def far_first(length):
    return sorted(range(1, length), key=lambda o: -min(o, length - o))


def dot_nt(a, b):
    return lax.dot_general(a, b, (((1,), (1,)), ((), ())), preferred_element_type=F32)


def dot_nn(a, b):
    return lax.dot_general(a, b, (((1,), (0,)), ((), ())), preferred_element_type=F32)


def remote(src, dst, send, recv, device):
    return pltpu.make_async_remote_copy(
        src_ref=src, dst_ref=dst, send_sem=send, recv_sem=recv,
        device_id=device, device_id_type=MESH,
    )


def make_kernel(sizes, blocks, tokens, hd, fh):
    ny, nx, nz = sizes
    half = fh // 2
    rows = 3 * half // ny
    cols = hd // nx
    wrows = hd // (nx * ny * 2)
    pieces = nx * ny

    def kernel(
        q_hbm, k_hbm, v_hbm, r_hbm, f_hbm, out_hbm,
        kbuf, dbuf, qbuf, vbuf, rbuf, dsrc, fpc, wag, gag, gsend, rx, ysend, ry,
        wf, wb, pbuf, obuf,
        zrecv, zsend, frecv, fsend, lsem, fpsem, xrecv, xsend, yrecv, ysem, arecv, asend,
    ):
        y, x, c, z = (lax.axis_index(a) for a in ("y", "x", "c", "z"))
        oc = 1 - c

        def at_y(o):
            return lax.rem(y + o, ny)

        def at_x(o):
            return lax.rem(x + o, nx)

        def at_z(o):
            return lax.rem(z + o, nz)

        barrier = pltpu.get_barrier_semaphore()
        greet = [{"z": at_z(o)} for o in range(1, nz)]
        greet += [{"x": at_x(o)} for o in range(1, nx)]
        greet += [{"y": at_y(o)} for o in range(1, ny)]
        greet += [{"c": oc}]

        load_v = pltpu.make_async_copy(v_hbm, vbuf, lsem.at[0])
        load_r = pltpu.make_async_copy(r_hbm, rbuf, lsem.at[1])
        load_f = pltpu.make_async_copy(
            f_hbm.at[0, :, :, pl.ds(pl.multiple_of(c * half, half), half)], fpc.at[c], lsem.at[2]
        )
        load_v.start()
        load_r.start()
        load_f.start()
        for device in greet:
            pl.semaphore_signal(barrier, inc=1, device_id=device, device_id_type=MESH)
        pl.semaphore_wait(barrier, len(greet))

        def head_columns(ref, b, t):
            return ref.at[b, :, pl.ds(pl.multiple_of(t * hd, hd), hd)]

        def z_send(kind, b, source, target):
            for o in far_first(nz):
                t = at_z(o)
                remote(source(t), target, zsend.at[kind, b], zrecv.at[kind, b, z], {"z": t}).start()
            pltpu.make_async_copy(source(z), target, zrecv.at[kind, b, z]).start()

        def z_wait(kind, b, target, zs):
            pltpu.make_async_copy(target, target, zrecv.at[kind, b, zs]).wait()

        def send_keys(b):
            z_send(0, b, lambda t: head_columns(k_hbm, b, t), kbuf.at[b, c, z])

        def send_grads(b):
            z_send(1, b, lambda t: dsrc.at[b, t], dbuf.at[b, c, z])

        def send_queries(b):
            z_send(2, b, lambda t: head_columns(q_hbm, b, t), qbuf.at[b, z])

        def scale_values(b):
            for h in range(nz):
                dsrc[b, h] = (
                    -(rbuf[b, :, h : h + 1].astype(F32) * vbuf[b, :, h * hd : (h + 1) * hd].astype(F32))
                ).astype(BF16)

        send_keys(0)
        f_copy = remote(
            f_hbm.at[0, :, :, pl.ds(pl.multiple_of(oc * half, half), half)],
            fpc.at[c], fpsem.at[0], fpsem.at[1], {"c": oc},
        )
        f_copy.start()
        load_v.wait()
        load_r.wait()
        scale_values(0)
        send_grads(0)

        def slot(cc, xx, yy):
            return (cc * nx + xx) * ny + yy

        def all_gather(which, buf):
            own = slot(c, x, y)
            send = asend.at[which]

            def give(s, device):
                remote(buf.at[s], buf.at[s], send, arecv.at[which, s], device).start()

            def take(s):
                remote(buf.at[s], buf.at[s], send, arecv.at[which, s], {"c": oc}).wait_recv()

            for o in far_first(ny):
                give(own, {"y": at_y(o)})
            for o in far_first(nx):
                give(own, {"x": at_x(o)})
            give(own, {"c": oc})
            for o in reversed(far_first(ny)):
                s = slot(c, x, at_y(o))
                take(s)
                for ox in far_first(nx):
                    give(s, {"x": at_x(ox)})
                give(s, {"c": oc})
            for o in [0] + list(reversed(far_first(ny))):
                for ox in reversed(far_first(nx)):
                    s = slot(c, at_x(ox), at_y(o))
                    take(s)
                    give(s, {"c": oc})
            for o in [0] + list(reversed(far_first(ny))):
                for ox in [0] + list(reversed(far_first(nx))):
                    take(slot(oc, at_x(ox), at_y(o)))

        load_f.wait()
        f_copy.wait_recv()
        wag[slot(c, x, y)] = jnp.concatenate([fpc[0], fpc[1]], axis=1).astype(BF16)
        all_gather(0, wag)
        for m in range(3):
            for cc in range(2):
                part = jnp.concatenate(
                    [wag[slot(cc, xx, yy), m] for yy in range(ny) for xx in range(nx)], axis=0
                )
                turned = part.T
                wb[m, cc] = turned
                wf[m, cc] = turned.astype(F32)

        for b in range(1, blocks):
            scale_values(b)

        def forward(b):
            for o in far_first(nz) + [0]:
                zs = lax.rem(z - o + nz, nz)
                for kind, buf in ((0, kbuf), (1, dbuf)):
                    mine = buf.at[b, c, zs]
                    z_wait(kind, b, mine, zs)
                    remote(
                        mine, mine, fsend.at[b, kind], frecv.at[b, kind, zs], {"c": oc}
                    ).start()

        def forwarded(b):
            for zs in range(nz):
                for kind, buf in ((0, kbuf), (1, dbuf)):
                    other = buf.at[b, oc, zs]
                    remote(other, other, fsend.at[b, kind], frecv.at[b, kind, zs], {"c": oc}).wait_recv()

        count = nz * tokens

        def hidden_parts(b, cc):
            keys = kbuf[b, cc].reshape(count, hd)
            out_grad = dbuf[b, cc].reshape(count, hd)
            gate_up = dot_nt(keys, jnp.concatenate([wb[0, c], wb[1, c]], axis=0))
            gate, up = gate_up[:, :half], gate_up[:, half:]
            hidden_grad = dot_nt(out_grad, wb[2, c])
            sig = jax.nn.sigmoid(gate)
            act = gate * sig
            slope = sig * (1.0 + gate * (1.0 - sig))
            at = pl.ds(pl.multiple_of(cc * count, count), count)
            pbuf[at, 0:half] = (hidden_grad * up * slope).astype(BF16)
            pbuf[at, half : 2 * half] = (hidden_grad * act).astype(BF16)
            pbuf[at, 2 * half : 3 * half] = (act * up).astype(BF16)

        def gradients(b):
            keys = kbuf[b].reshape(2 * count, hd)
            out_grad = dbuf[b].reshape(2 * count, hd)
            turned = pbuf[...].T
            both = jnp.concatenate(
                [dot_nn(turned[: 2 * half], keys), dot_nn(turned[2 * half :], out_grad)], axis=0
            )
            for xx in range(nx):
                gsend[b, xx] = both[:, xx * cols : (xx + 1) * cols].astype(BF16).reshape(ny, rows, cols)

        def start_reduce(b):
            for o in far_first(ny) + [0]:
                yr = at_y(o)
                for ox in far_first(nx):
                    xt = at_x(ox)
                    remote(
                        gsend.at[b, xt, yr], rx.at[b, ox - 1, yr],
                        xsend.at[b], xrecv.at[b, ox - 1, yr], {"x": xt},
                    ).start()

        def finish_reduce(b):
            total = None
            for o in far_first(ny) + [0]:
                yr = at_y(o)
                total = gsend[b, x, yr].astype(F32)
                for ox in range(1, nx):
                    land = rx.at[b, ox - 1, yr]
                    remote(land, land, xsend.at[b], xrecv.at[b, ox - 1, yr], {"c": oc}).wait_recv()
                    total = total + rx[b, ox - 1, yr].astype(F32)
                if o:
                    ysend[b, o - 1] = total.astype(BF16)
                    remote(
                        ysend.at[b, o - 1], ry.at[b, o - 1],
                        ysem.at[b], yrecv.at[b, o - 1], {"y": yr},
                    ).start()
            for o in far_first(ny):
                land = ry.at[b, o - 1]
                remote(land, land, ysem.at[b], yrecv.at[b, o - 1], {"c": oc}).wait_recv()
                total = total + ry[b, o - 1].astype(F32)
            gag[b, slot(c, x, y)] = total.astype(BF16)
            all_gather(1 + b, gag.at[b])

        def update(b):
            for m in range(3):
                low = jnp.concatenate(
                    [
                        jnp.concatenate(
                            [
                                gag[b, slot(cc, xx, 0) : slot(cc, xx, 0) + ny].reshape(3 * half, cols)[
                                    m * half : (m + 1) * half
                                ]
                                for xx in range(nx)
                            ],
                            axis=1,
                        )
                        for cc in range(2)
                    ],
                    axis=0,
                )
                full = low.astype(F32)
                inverse = 1.0 / (jnp.sqrt(jnp.sum(full * full, keepdims=True)) + EPSILON)
                gram = dot_nt(low, low) * (inverse * inverse)
                gram_low = gram.astype(BF16)
                poly = COEF_B * gram + COEF_C * dot_nn(gram_low, gram_low)
                first = (COEF_A * full + dot_nn(poly.astype(BF16), low)) * inverse
                first_low = first.astype(BF16)
                gram = dot_nt(first_low, first_low)
                gram_low = gram.astype(BF16)
                poly = COEF_B * gram + COEF_C * dot_nn(gram_low, gram_low)
                second = COEF_A * first + dot_nn(poly.astype(BF16), first_low)
                fresh = wf[m].reshape(fh, hd) - LEARNING_STEP * second
                wf[m] = fresh.reshape(2, half, hd)
                wb[m] = fresh.astype(BF16).reshape(2, half, hd)

        def out_copy(b):
            return pltpu.make_async_copy(obuf.at[b], out_hbm.at[b], lsem.at[3 + b])

        def answer(b):
            queries = qbuf[b].reshape(count, hd)
            gate = dot_nt(queries, wb[0].reshape(fh, hd))
            up = dot_nt(queries, wb[1].reshape(fh, hd))
            hidden = (gate * jax.nn.sigmoid(gate) * up).astype(BF16)
            obuf[b] = dot_nn(hidden, wb[2].reshape(fh, hd)).astype(BF16)
            out_copy(b).start()

        forward(0)
        for b in range(1, blocks):
            send_keys(b)
            send_grads(b)
        for b in range(blocks):
            send_queries(b)

        for b in range(blocks):
            hidden_parts(b, c)
            forwarded(b)
            hidden_parts(b, oc)
            gradients(b)
            start_reduce(b)
            if b:
                for zs in range(nz):
                    z_wait(2, b - 1, qbuf.at[b - 1, zs], zs)
                answer(b - 1)
            finish_reduce(b)
            if b + 1 < blocks:
                forward(b + 1)
            update(b)
        last = blocks - 1
        for zs in range(nz):
            z_wait(2, last, qbuf.at[last, zs], zs)
        answer(last)

        def sent(ref, sem):
            pltpu.make_async_copy(ref, ref, sem).wait()

        for b in range(blocks):
            for kind in range(3):
                sent(qbuf.at[0, 0 : nz - 1], zsend.at[kind, b])
            for kind in range(2):
                sent(kbuf.at[b, 0], fsend.at[b, kind])
            sent(gsend.at[b, 0 : nx - 1], xsend.at[b])
            sent(ysend.at[b], ysem.at[b])
            sent(gag.at[b, 0 : 2 * pieces - 1], asend.at[1 + b])
        sent(wag.at[0 : 2 * pieces - 1], asend.at[0])
        f_copy.wait_send()
        for b in range(blocks):
            out_copy(b).wait()

    dma = pltpu.SemaphoreType.DMA
    scratch = [
        pltpu.VMEM((blocks, 2, nz, tokens, hd), BF16),
        pltpu.VMEM((blocks, 2, nz, tokens, hd), BF16),
        pltpu.VMEM((blocks, nz, tokens, hd), BF16),
        pltpu.VMEM((blocks, tokens, nz * hd), BF16),
        pltpu.VMEM((blocks, tokens, nz), BF16),
        pltpu.VMEM((blocks, nz, tokens, hd), BF16),
        pltpu.VMEM((2, 3, wrows, half), F32),
        pltpu.VMEM((2 * pieces, 3, 2 * wrows, half), BF16),
        pltpu.VMEM((blocks, 2 * pieces, rows, cols), BF16),
        pltpu.VMEM((blocks, nx, ny, rows, cols), BF16),
        pltpu.VMEM((blocks, nx - 1, ny, rows, cols), BF16),
        pltpu.VMEM((blocks, ny - 1, rows, cols), BF16),
        pltpu.VMEM((blocks, ny - 1, rows, cols), BF16),
        pltpu.VMEM((3, 2, half, hd), F32),
        pltpu.VMEM((3, 2, half, hd), BF16),
        pltpu.VMEM((2 * nz * tokens, 3 * half), BF16),
        pltpu.VMEM((blocks, nz * tokens, hd), BF16),
        dma((3, blocks, nz)),
        dma((3, blocks)),
        dma((blocks, 2, nz)),
        dma((blocks, 2)),
        dma((3 + blocks,)),
        dma((2,)),
        dma((blocks, nx - 1, ny)),
        dma((blocks,)),
        dma((blocks, ny - 1)),
        dma((blocks,)),
        dma((1 + blocks, 2 * pieces)),
        dma((1 + blocks,)),
    ]
    return kernel, scratch


def build(mesh):
    ny, nx, _, nz = (mesh.shape[a] for a in ("y", "x", "c", "z"))

    def local(queries, keys, values, rates, fast_init):
        blocks, tokens, width = queries.shape
        hd = width // nz
        fh = fast_init.shape[3]
        kernel, scratch = make_kernel((ny, nx, nz), blocks, tokens, hd, fh)
        return pl.pallas_call(
            kernel,
            out_shape=jax.ShapeDtypeStruct((blocks, nz * tokens, hd), BF16),
            in_specs=[pl.BlockSpec(memory_space=pl.ANY)] * 5,
            out_specs=pl.BlockSpec(memory_space=pl.ANY),
            scratch_shapes=scratch,
            compiler_params=pltpu.CompilerParams(
                collective_id=0, has_side_effects=True, vmem_limit_bytes=60 * 1024 * 1024
            ),
        )(queries, keys, values, rates, fast_init)

    tokens_at = ("y", "x", "c", "z")
    in_specs = (
        P(None, tokens_at, None),
        P(None, tokens_at, None),
        P(None, tokens_at, None),
        P(None, tokens_at, None),
        P("z", None, ("y", "x", "c"), None),
    )
    out_specs = P(None, ("y", "x", "c"), "z")
    return jax.shard_map(local, mesh=mesh, in_specs=in_specs, out_specs=out_specs, check_vma=False)


def solution(mesh):
    seq, heads = mesh.shape["seq"], mesh.shape["head"]
    return build(Mesh(mesh.devices.reshape(seq // 8, 4, 2, heads), ("y", "x", "c", "z")))
```

```python
import jax
import jax.numpy as jnp
from jax import lax
from jax.experimental import pallas as pl
from jax.experimental.pallas import tpu as pltpu
from jax.sharding import Mesh
from jax.sharding import PartitionSpec as P

EPSILON = 1e-06
COEF_A = 3.4445
COEF_B = -4.775
COEF_C = 2.0315
LEARNING_STEP = 0.5
MESH = pl.DeviceIdType.MESH
BF16 = jnp.bfloat16
F32 = jnp.float32


def far_first(length):
    return sorted(range(1, length), key=lambda o: -min(o, length - o))


def dot_nt(a, b):
    return lax.dot_general(a, b, (((1,), (1,)), ((), ())), preferred_element_type=F32)


def dot_nn(a, b):
    return lax.dot_general(a, b, (((1,), (0,)), ((), ())), preferred_element_type=F32)


def remote(src, dst, send, recv, device):
    return pltpu.make_async_remote_copy(
        src_ref=src, dst_ref=dst, send_sem=send, recv_sem=recv,
        device_id=device, device_id_type=MESH,
    )


def make_kernel(sizes, blocks, tokens, hd, fh):
    ny, nx, nz = sizes
    half = fh // 2
    rows = 3 * half // ny
    cols = hd // nx
    wrows = hd // (nx * ny * 2)
    pieces = nx * ny

    def kernel(
        q_hbm, k_hbm, v_hbm, r_hbm, f_hbm, out_ref,
        kbuf, dbuf, qbuf, vbuf, rbuf, dsrc, fpc, wag, gag, gsend, rx, ysend, ry,
        wf, wb, pbuf,
        zrecv, zsend, frecv, fsend, lsem, fpsem, xrecv, xsend, yrecv, ysem, arecv, asend,
    ):
        y, x, c, z = (lax.axis_index(a) for a in ("y", "x", "c", "z"))
        oc = 1 - c

        def at_y(o):
            return lax.rem(y + o, ny)

        def at_x(o):
            return lax.rem(x + o, nx)

        def at_z(o):
            return lax.rem(z + o, nz)

        barrier = pltpu.get_barrier_semaphore()
        greet = [{"z": at_z(o)} for o in range(1, nz)]
        greet += [{"x": at_x(o)} for o in range(1, nx)]
        greet += [{"y": at_y(o)} for o in range(1, ny)]
        greet += [{"c": oc}]

        load_v = pltpu.make_async_copy(v_hbm, vbuf, lsem.at[0])
        load_r = pltpu.make_async_copy(r_hbm, rbuf, lsem.at[1])
        load_f = pltpu.make_async_copy(
            f_hbm.at[0, :, :, pl.ds(pl.multiple_of(c * half, half), half)], fpc.at[c], lsem.at[2]
        )
        load_v.start()
        load_r.start()
        load_f.start()
        for device in greet:
            pl.semaphore_signal(barrier, inc=1, device_id=device, device_id_type=MESH)
        pl.semaphore_wait(barrier, len(greet))

        def head_columns(ref, b, t):
            return ref.at[b, :, pl.ds(pl.multiple_of(t * hd, hd), hd)]

        def z_send(kind, b, source, target):
            for o in far_first(nz):
                t = at_z(o)
                remote(source(t), target, zsend.at[kind, b], zrecv.at[kind, b, z], {"z": t}).start()
            pltpu.make_async_copy(source(z), target, zrecv.at[kind, b, z]).start()

        def z_wait(kind, b, target, zs):
            pltpu.make_async_copy(target, target, zrecv.at[kind, b, zs]).wait()

        def send_keys(b):
            z_send(0, b, lambda t: head_columns(k_hbm, b, t), kbuf.at[b, c, z])

        def send_grads(b):
            z_send(1, b, lambda t: dsrc.at[b, t], dbuf.at[b, c, z])

        def send_queries(b):
            z_send(2, b, lambda t: head_columns(q_hbm, b, t), qbuf.at[b, z])

        def scale_values(b):
            rate = rbuf[b].astype(F32).T
            for h in range(nz):
                dsrc[b, h] = (
                    -(rate[:, h : h + 1] * vbuf[b, :, h * hd : (h + 1) * hd].astype(F32))
                ).astype(BF16)

        send_keys(0)
        f_copy = remote(
            f_hbm.at[0, :, :, pl.ds(pl.multiple_of(oc * half, half), half)],
            fpc.at[c], fpsem.at[0], fpsem.at[1], {"c": oc},
        )
        f_copy.start()
        load_v.wait()
        load_r.wait()
        scale_values(0)
        send_grads(0)

        def slot(cc, xx, yy):
            return (cc * nx + xx) * ny + yy

        def all_gather(which, buf):
            own = slot(c, x, y)
            send = asend.at[which]

            def give(s, device):
                remote(buf.at[s], buf.at[s], send, arecv.at[which, s], device).start()

            def take(s):
                remote(buf.at[s], buf.at[s], send, arecv.at[which, s], {"c": oc}).wait_recv()

            for o in far_first(ny):
                give(own, {"y": at_y(o)})
            for o in far_first(nx):
                give(own, {"x": at_x(o)})
            give(own, {"c": oc})
            for o in reversed(far_first(ny)):
                s = slot(c, x, at_y(o))
                take(s)
                for ox in far_first(nx):
                    give(s, {"x": at_x(ox)})
                give(s, {"c": oc})
            for o in [0] + list(reversed(far_first(ny))):
                for ox in reversed(far_first(nx)):
                    s = slot(c, at_x(ox), at_y(o))
                    take(s)
                    give(s, {"c": oc})
            for o in [0] + list(reversed(far_first(ny))):
                for ox in [0] + list(reversed(far_first(nx))):
                    take(slot(oc, at_x(ox), at_y(o)))

        load_f.wait()
        f_copy.wait_recv()
        wag[slot(c, x, y)] = jnp.concatenate([fpc[0], fpc[1]], axis=1).astype(BF16)
        all_gather(0, wag)
        for m in range(3):
            for cc in range(2):
                part = jnp.concatenate(
                    [wag[slot(cc, xx, yy), m] for yy in range(ny) for xx in range(nx)], axis=0
                )
                turned = part.T
                wb[m, cc] = turned
                wf[m, cc] = turned.astype(F32)

        for b in range(1, blocks):
            scale_values(b)

        def forward(b):
            for o in far_first(nz) + [0]:
                zs = lax.rem(z - o + nz, nz)
                for kind, buf in ((0, kbuf), (1, dbuf)):
                    mine = buf.at[b, c, zs]
                    z_wait(kind, b, mine, zs)
                    remote(
                        mine, mine, fsend.at[b, kind], frecv.at[b, kind, zs], {"c": oc}
                    ).start()

        def forwarded(b):
            for zs in range(nz):
                for kind, buf in ((0, kbuf), (1, dbuf)):
                    other = buf.at[b, oc, zs]
                    remote(other, other, fsend.at[b, kind], frecv.at[b, kind, zs], {"c": oc}).wait_recv()

        count = nz * tokens

        def hidden_parts(b, cc):
            keys = kbuf[b, cc].reshape(count, hd)
            out_grad = dbuf[b, cc].reshape(count, hd)
            gate_up = dot_nt(keys, jnp.concatenate([wb[0, c], wb[1, c]], axis=0))
            gate, up = gate_up[:, :half], gate_up[:, half:]
            hidden_grad = dot_nt(out_grad, wb[2, c])
            sig = jax.nn.sigmoid(gate)
            act = gate * sig
            slope = sig * (1.0 + gate * (1.0 - sig))
            at = pl.ds(pl.multiple_of(cc * count, count), count)
            pbuf[at, 0:half] = (hidden_grad * up * slope).astype(BF16)
            pbuf[at, half : 2 * half] = (hidden_grad * act).astype(BF16)
            pbuf[at, 2 * half : 3 * half] = (act * up).astype(BF16)

        def gradients(b):
            keys = kbuf[b].reshape(2 * count, hd)
            out_grad = dbuf[b].reshape(2 * count, hd)
            turned = pbuf[...].T
            both = jnp.concatenate(
                [dot_nn(turned[: 2 * half], keys), dot_nn(turned[2 * half :], out_grad)], axis=0
            )
            for xx in range(nx):
                gsend[b, xx] = both[:, xx * cols : (xx + 1) * cols].astype(BF16).reshape(ny, rows, cols)

        def start_reduce(b):
            for o in far_first(ny) + [0]:
                yr = at_y(o)
                for ox in far_first(nx):
                    xt = at_x(ox)
                    remote(
                        gsend.at[b, xt, yr], rx.at[b, ox - 1, yr],
                        xsend.at[b], xrecv.at[b, ox - 1, yr], {"x": xt},
                    ).start()

        def finish_reduce(b):
            total = None
            for o in far_first(ny) + [0]:
                yr = at_y(o)
                total = gsend[b, x, yr].astype(F32)
                for ox in range(1, nx):
                    land = rx.at[b, ox - 1, yr]
                    remote(land, land, xsend.at[b], xrecv.at[b, ox - 1, yr], {"c": oc}).wait_recv()
                    total = total + rx[b, ox - 1, yr].astype(F32)
                if o:
                    ysend[b, o - 1] = total.astype(BF16)
                    remote(
                        ysend.at[b, o - 1], ry.at[b, o - 1],
                        ysem.at[b], yrecv.at[b, o - 1], {"y": yr},
                    ).start()
            for o in far_first(ny):
                land = ry.at[b, o - 1]
                remote(land, land, ysem.at[b], yrecv.at[b, o - 1], {"c": oc}).wait_recv()
                total = total + ry[b, o - 1].astype(F32)
            gag[b, slot(c, x, y)] = total.astype(BF16)
            all_gather(1 + b, gag.at[b])

        def update(b):
            lows = []
            for m in range(3):
                halves = []
                for cc in range(2):
                    parts = []
                    for xx in range(nx):
                        first_slot = slot(cc, xx, 0)
                        whole = gag[b, first_slot : first_slot + ny].reshape(3 * half, cols)
                        parts.append(whole[m * half : (m + 1) * half])
                    halves.append(jnp.concatenate(parts, axis=1))
                lows.append(jnp.concatenate(halves, axis=0))
            grams = [dot_nt(low, low) for low in lows]
            inverses = []
            for low in lows:
                full = low.astype(F32)
                inverses.append(1.0 / (jnp.sqrt(jnp.sum(full * full, keepdims=True)) + EPSILON))
            grams = [g * (i * i) for g, i in zip(grams, inverses)]
            polys = [COEF_B * g + COEF_C * dot_nn(g.astype(BF16), g.astype(BF16)) for g in grams]
            firsts = [
                (COEF_A * low.astype(F32) + dot_nn(p.astype(BF16), low)) * i
                for low, p, i in zip(lows, polys, inverses)
            ]
            first_lows = [f.astype(BF16) for f in firsts]
            grams = [dot_nt(f, f) for f in first_lows]
            polys = [COEF_B * g + COEF_C * dot_nn(g.astype(BF16), g.astype(BF16)) for g in grams]
            for m in range(3):
                second = COEF_A * firsts[m] + dot_nn(polys[m].astype(BF16), first_lows[m])
                fresh = wf[m].reshape(fh, hd) - LEARNING_STEP * second
                wf[m] = fresh.reshape(2, half, hd)
                wb[m] = fresh.astype(BF16).reshape(2, half, hd)

        def answer(b):
            queries = qbuf[b].reshape(count, hd)
            gate = dot_nt(queries, wb[0].reshape(fh, hd))
            up = dot_nt(queries, wb[1].reshape(fh, hd))
            hidden = (gate * jax.nn.sigmoid(gate) * up).astype(BF16)
            out_ref[b] = dot_nn(hidden, wb[2].reshape(fh, hd)).astype(BF16)

        forward(0)
        for b in range(1, blocks):
            send_keys(b)
            send_grads(b)
        for b in range(blocks):
            send_queries(b)

        for b in range(blocks):
            hidden_parts(b, c)
            forwarded(b)
            hidden_parts(b, oc)
            gradients(b)
            start_reduce(b)
            if b:
                for zs in range(nz):
                    z_wait(2, b - 1, qbuf.at[b - 1, zs], zs)
                answer(b - 1)
            finish_reduce(b)
            if b + 1 < blocks:
                forward(b + 1)
            update(b)
        last = blocks - 1
        for zs in range(nz):
            z_wait(2, last, qbuf.at[last, zs], zs)
        answer(last)

        def sent(ref, sem):
            pltpu.make_async_copy(ref, ref, sem).wait()

        for b in range(blocks):
            for kind in range(3):
                sent(qbuf.at[0, 0 : nz - 1], zsend.at[kind, b])
            for kind in range(2):
                sent(kbuf.at[b, 0], fsend.at[b, kind])
            sent(gsend.at[b, 0 : nx - 1], xsend.at[b])
            sent(ysend.at[b], ysem.at[b])
            sent(gag.at[b, 0 : 2 * pieces - 1], asend.at[1 + b])
        sent(wag.at[0 : 2 * pieces - 1], asend.at[0])
        f_copy.wait_send()

    dma = pltpu.SemaphoreType.DMA
    scratch = [
        pltpu.VMEM((blocks, 2, nz, tokens, hd), BF16),
        pltpu.VMEM((blocks, 2, nz, tokens, hd), BF16),
        pltpu.VMEM((blocks, nz, tokens, hd), BF16),
        pltpu.VMEM((blocks, tokens, nz * hd), BF16),
        pltpu.VMEM((blocks, nz, tokens), BF16),
        pltpu.VMEM((blocks, nz, tokens, hd), BF16),
        pltpu.VMEM((2, 3, wrows, half), F32),
        pltpu.VMEM((2 * pieces, 3, 2 * wrows, half), BF16),
        pltpu.VMEM((blocks, 2 * pieces, rows, cols), BF16),
        pltpu.VMEM((blocks, nx, ny, rows, cols), BF16),
        pltpu.VMEM((blocks, nx - 1, ny, rows, cols), BF16),
        pltpu.VMEM((blocks, ny - 1, rows, cols), BF16),
        pltpu.VMEM((blocks, ny - 1, rows, cols), BF16),
        pltpu.VMEM((3, 2, half, hd), F32),
        pltpu.VMEM((3, 2, half, hd), BF16),
        pltpu.VMEM((2 * nz * tokens, 3 * half), BF16),
        dma((3, blocks, nz)),
        dma((3, blocks)),
        dma((blocks, 2, nz)),
        dma((blocks, 2)),
        dma((3,)),
        dma((2,)),
        dma((blocks, nx - 1, ny)),
        dma((blocks,)),
        dma((blocks, ny - 1)),
        dma((blocks,)),
        dma((1 + blocks, 2 * pieces)),
        dma((1 + blocks,)),
    ]
    return kernel, scratch


def build(mesh):
    ny, nx, _, nz = (mesh.shape[a] for a in ("y", "x", "c", "z"))

    def local(queries, keys, values, rates, fast_init):
        blocks, tokens, width = queries.shape
        hd = width // nz
        fh = fast_init.shape[3]
        kernel, scratch = make_kernel((ny, nx, nz), blocks, tokens, hd, fh)
        return pl.pallas_call(
            kernel,
            out_shape=pltpu.VMEM((blocks, nz * tokens, hd), BF16),
            in_specs=[pl.BlockSpec(memory_space=pl.ANY)] * 5,
            out_specs=pl.BlockSpec(memory_space=pltpu.VMEM),
            scratch_shapes=scratch,
            compiler_params=pltpu.CompilerParams(
                collective_id=0, has_side_effects=True, vmem_limit_bytes=60 * 1024 * 1024
            ),
        )(queries, keys, values, jnp.swapaxes(rates, 1, 2), fast_init)

    tokens_at = ("y", "x", "c", "z")
    in_specs = (
        P(None, tokens_at, None),
        P(None, tokens_at, None),
        P(None, tokens_at, None),
        P(None, tokens_at, None),
        P("z", None, ("y", "x", "c"), None),
    )
    out_specs = P(None, ("y", "x", "c"), "z")
    return jax.shard_map(local, mesh=mesh, in_specs=in_specs, out_specs=out_specs, check_vma=False)


def solution(mesh):
    seq, heads = mesh.shape["seq"], mesh.shape["head"]
    return build(Mesh(mesh.devices.reshape(seq // 8, 4, 2, heads), ("y", "x", "c", "z")))
```

```python
import jax
import jax.numpy as jnp
from jax import lax
from jax.experimental import pallas as pl
from jax.experimental.pallas import tpu as pltpu
from jax.sharding import Mesh
from jax.sharding import PartitionSpec as P

EPSILON = 1e-06
COEF_A = 3.4445
COEF_B = -4.775
COEF_C = 2.0315
LEARNING_STEP = 0.5
MESH = pl.DeviceIdType.MESH
BF16 = jnp.bfloat16
F32 = jnp.float32


def far_first(length):
    return sorted(range(1, length), key=lambda o: -min(o, length - o))


def dot_nt(a, b):
    return lax.dot_general(a, b, (((1,), (1,)), ((), ())), preferred_element_type=F32)


def dot_nn(a, b):
    return lax.dot_general(a, b, (((1,), (0,)), ((), ())), preferred_element_type=F32)


def remote(src, dst, send, recv, device):
    return pltpu.make_async_remote_copy(
        src_ref=src, dst_ref=dst, send_sem=send, recv_sem=recv,
        device_id=device, device_id_type=MESH,
    )


def make_kernel(sizes, blocks, tokens, hd, fh):
    ny, nx, nz = sizes
    half = fh // 2
    rows = 2 * half // ny
    rest = half // ny
    cols = hd // nx
    wrows = hd // (nx * ny * 2)
    pieces = nx * ny

    def kernel(
        q_hbm, k_hbm, v_hbm, r_hbm, f_hbm, out_ref,
        kbuf, dbuf, qbuf, vbuf, rbuf, dsrc, fpc, wag,
        a_send, a_land, a_send2, a_land2, a_all,
        b_send, b_land, b_send2, b_land2, b_all,
        wf, wb, pbuf, acts, slopes,
        zrecv, zsend, frecv, fsend, lsem, fpsem, wrecv, wsend,
        a_recv1, a_sem1, a_recv2, a_sem2, a_recv3, a_sem3,
        b_recv1, b_sem1, b_recv2, b_sem2, b_recv3, b_sem3,
    ):
        y, x, c, z = (lax.axis_index(a) for a in ("y", "x", "c", "z"))
        oc = 1 - c

        def at_y(o):
            return lax.rem(y + o, ny)

        def at_x(o):
            return lax.rem(x + o, nx)

        def at_z(o):
            return lax.rem(z + o, nz)

        barrier = pltpu.get_barrier_semaphore()
        greet = [{"z": at_z(o)} for o in range(1, nz)]
        greet += [{"x": at_x(o)} for o in range(1, nx)]
        greet += [{"y": at_y(o)} for o in range(1, ny)]
        greet += [{"c": oc}]

        load_v = pltpu.make_async_copy(v_hbm, vbuf, lsem.at[0])
        load_r = pltpu.make_async_copy(r_hbm, rbuf, lsem.at[1])
        load_f = pltpu.make_async_copy(
            f_hbm.at[0, :, :, pl.ds(pl.multiple_of(c * half, half), half)], fpc.at[c], lsem.at[2]
        )
        load_v.start()
        load_r.start()
        load_f.start()
        for device in greet:
            pl.semaphore_signal(barrier, inc=1, device_id=device, device_id_type=MESH)
        pl.semaphore_wait(barrier, len(greet))

        def head_columns(ref, b, t):
            return ref.at[b, :, pl.ds(pl.multiple_of(t * hd, hd), hd)]

        def z_send(kind, b, source, target):
            for o in far_first(nz):
                t = at_z(o)
                remote(source(t), target, zsend.at[kind, b], zrecv.at[kind, b, z], {"z": t}).start()
            pltpu.make_async_copy(source(z), target, zrecv.at[kind, b, z]).start()

        def z_wait(kind, b, target, zs):
            pltpu.make_async_copy(target, target, zrecv.at[kind, b, zs]).wait()

        def send_keys(b):
            z_send(0, b, lambda t: head_columns(k_hbm, b, t), kbuf.at[b, c, z])

        def send_grads(b):
            z_send(1, b, lambda t: dsrc.at[b, t], dbuf.at[b, c, z])

        def send_queries(b):
            z_send(2, b, lambda t: head_columns(q_hbm, b, t), qbuf.at[b, z])

        def scale_values(b):
            rate = rbuf[b].astype(F32).T
            for h in range(nz):
                dsrc[b, h] = (
                    -(rate[:, h : h + 1] * vbuf[b, :, h * hd : (h + 1) * hd].astype(F32))
                ).astype(BF16)

        send_keys(0)
        f_copy = remote(
            f_hbm.at[0, :, :, pl.ds(pl.multiple_of(oc * half, half), half)],
            fpc.at[c], fpsem.at[0], fpsem.at[1], {"c": oc},
        )
        f_copy.start()

        def slot(cc, xx, yy):
            return (cc * nx + xx) * ny + yy

        def across_y(o):
            return {"y": at_y(o)}

        def across_x(o):
            return {"x": at_x(o)}

        def slot_y(cc, oy, ox):
            return slot(cc, at_x(ox), at_y(oy))

        def slot_x(cc, ox, oy):
            return slot(cc, at_x(ox), at_y(oy))

        class Gather:
            def __init__(self, buf, send, recv, n1, peer1, n2, peer2, place):
                self.buf, self.send, self.recv, self.place = buf, send, recv, place
                self.n1, self.peer1, self.n2, self.peer2 = n1, peer1, n2, peer2
                self.own = place(c, 0, 0)

            def give(self, s, device):
                remote(self.buf.at[s], self.buf.at[s], self.send, self.recv.at[s], device).start()

            def take(self, s):
                remote(self.buf.at[s], self.buf.at[s], self.send, self.recv.at[s], {"c": oc}).wait_recv()

            def start1(self):
                for o in far_first(self.n1):
                    self.give(self.own, self.peer1(o))

            def start2(self):
                for o in far_first(self.n2):
                    self.give(self.own, self.peer2(o))
                self.give(self.own, {"c": oc})

            def relay1(self):
                for o in reversed(far_first(self.n1)):
                    s = self.place(c, o, 0)
                    self.take(s)
                    for o2 in far_first(self.n2):
                        self.give(s, self.peer2(o2))
                    self.give(s, {"c": oc})
                    yield

            def relay2(self):
                for o in [0] + list(reversed(far_first(self.n1))):
                    for o2 in reversed(far_first(self.n2)):
                        s = self.place(c, o, o2)
                        self.take(s)
                        self.give(s, {"c": oc})
                        yield

            def end(self):
                for o in [0] + list(reversed(far_first(self.n1))):
                    for o2 in [0] + list(reversed(far_first(self.n2))):
                        self.take(self.place(oc, o, o2))

        def run(*pairs):
            live = list(pairs)
            while live:
                for pair in list(live):
                    steps, many = pair
                    for _ in range(many):
                        try:
                            next(steps)
                        except StopIteration:
                            live.remove(pair)
                            break

        load_f.wait()
        f_copy.wait_recv()
        wag[slot(c, x, y)] = jnp.concatenate([fpc[0], fpc[1]], axis=1).astype(BF16)
        weights_gather = Gather(wag, wsend, wrecv, ny, across_y, nx, across_x, slot_y)
        weights_gather.start1()
        weights_gather.start2()
        load_v.wait()
        load_r.wait()
        scale_values(0)
        send_grads(0)
        run((weights_gather.relay1(), 1))
        run((weights_gather.relay2(), 1))

        def forward(b, kind, buf):
            for o in far_first(nz) + [0]:
                zs = lax.rem(z - o + nz, nz)
                mine = buf.at[b, c, zs]
                z_wait(kind, b, mine, zs)
                remote(mine, mine, fsend.at[b, kind], frecv.at[b, kind, zs], {"c": oc}).start()

        def forwarded(b, kind, buf):
            for zs in range(nz):
                other = buf.at[b, oc, zs]
                remote(other, other, fsend.at[b, kind], frecv.at[b, kind, zs], {"c": oc}).wait_recv()

        count = nz * tokens

        def keys_part(b, cc):
            keys = kbuf[b, cc].reshape(count, hd)
            gate_up = dot_nt(keys, jnp.concatenate([wb[0, c], wb[1, c]], axis=0))
            gate, up = gate_up[:, :half], gate_up[:, half:]
            sig = jax.nn.sigmoid(gate)
            act = gate * sig
            acts[cc] = act
            slopes[cc] = up * (sig * (1.0 + gate * (1.0 - sig)))
            pbuf[cc, :, 2 * half : 3 * half] = (act * up).astype(BF16)

        def grads_part(b, cc):
            hidden_grad = dot_nt(dbuf[b, cc].reshape(count, hd), wb[2, c])
            pbuf[cc, :, 0:half] = (hidden_grad * slopes[cc]).astype(BF16)
            pbuf[cc, :, half : 2 * half] = (hidden_grad * acts[cc]).astype(BF16)

        forward(0, 0, kbuf)
        weights_gather.end()
        for m in range(3):
            for cc in range(2):
                part = jnp.concatenate(
                    [wag[slot(cc, xx, yy), m] for yy in range(ny) for xx in range(nx)], axis=0
                )
                turned = part.T
                wb[m, cc] = turned
                wf[m, cc] = turned.astype(F32)
        keys_part(0, c)
        forwarded(0, 0, kbuf)
        keys_part(0, oc)
        forward(0, 1, dbuf)

        def gradients(b):
            keys = kbuf[b].reshape(2 * count, hd)
            out_grad = dbuf[b].reshape(2 * count, hd)
            turned = pbuf[...].reshape(2 * count, 3 * half).T
            third = dot_nn(turned[2 * half :], out_grad)
            for xx in range(nx):
                b_send[b, :, xx] = third[:, xx * cols : (xx + 1) * cols].astype(BF16).reshape(ny, rest, cols)
            both = dot_nn(turned[: 2 * half], keys)
            for xx in range(nx):
                a_send[b, xx] = both[:, xx * cols : (xx + 1) * cols].astype(BF16).reshape(ny, rows, cols)

        class Reduce:
            def __init__(self, b, bufs, sems, n1, at1, name1, me1, n2, at2, name2):
                self.send, self.land, self.send2, self.land2 = (r.at[b] for r in bufs)
                self.recv1, self.sem1, self.recv2, self.sem2 = (r.at[b] for r in sems)
                self.n1, self.at1, self.name1, self.me1 = n1, at1, name1, me1
                self.n2, self.at2, self.name2 = n2, at2, name2

            def start(self):
                for o in far_first(self.n2) + [0]:
                    end = self.at2(o)
                    for o1 in far_first(self.n1):
                        t = self.at1(o1)
                        remote(
                            self.send.at[t, end], self.land.at[o1 - 1, end],
                            self.sem1, self.recv1.at[o1 - 1, end], {self.name1: t},
                        ).start()

            def steps(self, result, where):
                total = None
                for o in far_first(self.n2) + [0]:
                    end = self.at2(o)
                    total = self.send[self.me1, end].astype(F32)
                    for o1 in range(1, self.n1):
                        land = self.land.at[o1 - 1, end]
                        remote(land, land, self.sem1, self.recv1.at[o1 - 1, end], {"c": oc}).wait_recv()
                        total = total + land[...].astype(F32)
                    if o:
                        self.send2[o - 1] = total.astype(BF16)
                        remote(
                            self.send2.at[o - 1], self.land2.at[o - 1],
                            self.sem2, self.recv2.at[o - 1], {self.name2: end},
                        ).start()
                    yield
                for o in far_first(self.n2):
                    land = self.land2.at[o - 1]
                    remote(land, land, self.sem2, self.recv2.at[o - 1], {"c": oc}).wait_recv()
                    total = total + land[...].astype(F32)
                    yield
                result[where] = total.astype(BF16)

        def sums(b):
            return (
                Reduce(
                    b, (a_send, a_land, a_send2, a_land2), (a_recv1, a_sem1, a_recv2, a_sem2),
                    nx, at_x, "x", x, ny, at_y, "y",
                ),
                Reduce(
                    b, (b_send, b_land, b_send2, b_land2), (b_recv1, b_sem1, b_recv2, b_sem2),
                    ny, at_y, "y", y, nx, at_x, "x",
                ),
            )

        def start_reduce(b):
            for part in reversed(sums(b)):
                part.start()

        def finish_reduce(b):
            first, second = sums(b)
            own = slot(c, x, y)
            run((first.steps(a_all.at[b], own), 2), (second.steps(b_all.at[b], own), 1))
            ga = Gather(a_all.at[b], a_sem3.at[b], a_recv3.at[b], ny, across_y, nx, across_x, slot_y)
            gb = Gather(b_all.at[b], b_sem3.at[b], b_recv3.at[b], nx, across_x, ny, across_y, slot_x)
            ga.start1()
            gb.start1()
            ga.start2()
            gb.start2()
            run((gb.relay1(), 1))
            run((ga.relay1(), 1))
            run((ga.relay2(), 1), (gb.relay2(), 1))
            ga.end()
            gb.end()

        def update(b):
            lows = []
            for m in range(3):
                halves = []
                for cc in range(2):
                    parts = []
                    for xx in range(nx):
                        first_slot = slot(cc, xx, 0)
                        if m < 2:
                            whole = a_all[b, first_slot : first_slot + ny].reshape(2 * half, cols)
                            parts.append(whole[m * half : (m + 1) * half])
                        else:
                            parts.append(b_all[b, first_slot : first_slot + ny].reshape(half, cols))
                    halves.append(jnp.concatenate(parts, axis=1))
                lows.append(jnp.concatenate(halves, axis=0))
            grams = [dot_nt(low, low) for low in lows]
            inverses = []
            for low in lows:
                full = low.astype(F32)
                inverses.append(1.0 / (jnp.sqrt(jnp.sum(full * full, keepdims=True)) + EPSILON))
            grams = [g * (i * i) for g, i in zip(grams, inverses)]
            polys = [COEF_B * g + COEF_C * dot_nn(g.astype(BF16), g.astype(BF16)) for g in grams]
            firsts = [
                (COEF_A * low.astype(F32) + dot_nn(p.astype(BF16), low)) * i
                for low, p, i in zip(lows, polys, inverses)
            ]
            first_lows = [f.astype(BF16) for f in firsts]
            grams = [dot_nt(f, f) for f in first_lows]
            polys = [COEF_B * g + COEF_C * dot_nn(g.astype(BF16), g.astype(BF16)) for g in grams]
            for m in range(3):
                second = COEF_A * firsts[m] + dot_nn(polys[m].astype(BF16), first_lows[m])
                fresh = wf[m].reshape(fh, hd) - LEARNING_STEP * second
                wf[m] = fresh.reshape(2, half, hd)
                wb[m] = fresh.astype(BF16).reshape(2, half, hd)

        def answer(b):
            queries = qbuf[b].reshape(count, hd)
            gate = dot_nt(queries, wb[0].reshape(fh, hd))
            up = dot_nt(queries, wb[1].reshape(fh, hd))
            hidden = (gate * jax.nn.sigmoid(gate) * up).astype(BF16)
            out_ref[b] = dot_nn(hidden, wb[2].reshape(fh, hd)).astype(BF16)

        for b in range(1, blocks):
            send_keys(b)

        for b in range(blocks):
            grads_part(b, c)
            forwarded(b, 1, dbuf)
            grads_part(b, oc)
            gradients(b)
            start_reduce(b)
            if b == 0:
                for later in range(1, blocks):
                    scale_values(later)
                    send_grads(later)
                for each in range(blocks):
                    send_queries(each)
            else:
                for zs in range(nz):
                    z_wait(2, b - 1, qbuf.at[b - 1, zs], zs)
                answer(b - 1)
            finish_reduce(b)
            if b + 1 < blocks:
                forward(b + 1, 0, kbuf)
                forward(b + 1, 1, dbuf)
            update(b)
            if b + 1 < blocks:
                keys_part(b + 1, c)
                forwarded(b + 1, 0, kbuf)
                keys_part(b + 1, oc)
        last = blocks - 1
        for zs in range(nz):
            z_wait(2, last, qbuf.at[last, zs], zs)
        answer(last)

        def sent(ref, sem):
            pltpu.make_async_copy(ref, ref, sem).wait()

        for b in range(blocks):
            for kind in range(3):
                sent(qbuf.at[0, 0 : nz - 1], zsend.at[kind, b])
            for kind in range(2):
                sent(kbuf.at[b, 0], fsend.at[b, kind])
            sent(a_send.at[b, 0 : nx - 1], a_sem1.at[b])
            sent(b_send.at[b, 0 : ny - 1], b_sem1.at[b])
            sent(a_send2.at[b], a_sem2.at[b])
            sent(b_send2.at[b], b_sem2.at[b])
            sent(a_all.at[b, 0 : 2 * pieces - 1], a_sem3.at[b])
            sent(b_all.at[b, 0 : 2 * pieces - 1], b_sem3.at[b])
        sent(wag.at[0 : 2 * pieces - 1], wsend)
        f_copy.wait_send()

    dma = pltpu.SemaphoreType.DMA
    scratch = [
        pltpu.VMEM((blocks, 2, nz, tokens, hd), BF16),
        pltpu.VMEM((blocks, 2, nz, tokens, hd), BF16),
        pltpu.VMEM((blocks, nz, tokens, hd), BF16),
        pltpu.VMEM((blocks, tokens, nz * hd), BF16),
        pltpu.VMEM((blocks, nz, tokens), BF16),
        pltpu.VMEM((blocks, nz, tokens, hd), BF16),
        pltpu.VMEM((2, 3, wrows, half), F32),
        pltpu.VMEM((2 * pieces, 3, 2 * wrows, half), BF16),
        pltpu.VMEM((blocks, nx, ny, rows, cols), BF16),
        pltpu.VMEM((blocks, nx - 1, ny, rows, cols), BF16),
        pltpu.VMEM((blocks, ny - 1, rows, cols), BF16),
        pltpu.VMEM((blocks, ny - 1, rows, cols), BF16),
        pltpu.VMEM((blocks, 2 * pieces, rows, cols), BF16),
        pltpu.VMEM((blocks, ny, nx, rest, cols), BF16),
        pltpu.VMEM((blocks, ny - 1, nx, rest, cols), BF16),
        pltpu.VMEM((blocks, nx - 1, rest, cols), BF16),
        pltpu.VMEM((blocks, nx - 1, rest, cols), BF16),
        pltpu.VMEM((blocks, 2 * pieces, rest, cols), BF16),
        pltpu.VMEM((3, 2, half, hd), F32),
        pltpu.VMEM((3, 2, half, hd), BF16),
        pltpu.VMEM((2, nz * tokens, 3 * half), BF16),
        pltpu.VMEM((2, nz * tokens, half), F32),
        pltpu.VMEM((2, nz * tokens, half), F32),
        dma((3, blocks, nz)),
        dma((3, blocks)),
        dma((blocks, 2, nz)),
        dma((blocks, 2)),
        dma((3,)),
        dma((2,)),
        dma((2 * pieces,)),
        dma(()),
        dma((blocks, nx - 1, ny)),
        dma((blocks,)),
        dma((blocks, ny - 1)),
        dma((blocks,)),
        dma((blocks, 2 * pieces)),
        dma((blocks,)),
        dma((blocks, ny - 1, nx)),
        dma((blocks,)),
        dma((blocks, nx - 1)),
        dma((blocks,)),
        dma((blocks, 2 * pieces)),
        dma((blocks,)),
    ]
    return kernel, scratch


def build(mesh):
    ny, nx, _, nz = (mesh.shape[a] for a in ("y", "x", "c", "z"))

    def local(queries, keys, values, rates, fast_init):
        blocks, tokens, width = queries.shape
        hd = width // nz
        fh = fast_init.shape[3]
        kernel, scratch = make_kernel((ny, nx, nz), blocks, tokens, hd, fh)
        return pl.pallas_call(
            kernel,
            out_shape=pltpu.VMEM((blocks, nz * tokens, hd), BF16),
            in_specs=[pl.BlockSpec(memory_space=pl.ANY)] * 5,
            out_specs=pl.BlockSpec(memory_space=pltpu.VMEM),
            scratch_shapes=scratch,
            compiler_params=pltpu.CompilerParams(
                collective_id=0, has_side_effects=True, vmem_limit_bytes=60 * 1024 * 1024
            ),
        )(queries, keys, values, jnp.swapaxes(rates, 1, 2), fast_init)

    tokens_at = ("y", "x", "c", "z")
    in_specs = (
        P(None, tokens_at, None),
        P(None, tokens_at, None),
        P(None, tokens_at, None),
        P(None, tokens_at, None),
        P("z", None, ("y", "x", "c"), None),
    )
    out_specs = P(None, ("y", "x", "c"), "z")
    return jax.shard_map(local, mesh=mesh, in_specs=in_specs, out_specs=out_specs, check_vma=False)


def solution(mesh):
    seq, heads = mesh.shape["seq"], mesh.shape["head"]
    return build(Mesh(mesh.devices.reshape(seq // 8, 4, 2, heads), ("y", "x", "c", "z")))
```

```python
import jax
import jax.numpy as jnp
from jax import lax
from jax.experimental import pallas as pl
from jax.experimental.pallas import tpu as pltpu
from jax.sharding import Mesh
from jax.sharding import PartitionSpec as P

EPSILON = 1e-06
COEF_A = 3.4445
COEF_B = -4.775
COEF_C = 2.0315
LEARNING_STEP = 0.5
MESH = pl.DeviceIdType.MESH
BF16 = jnp.bfloat16
F32 = jnp.float32


def far_first(length):
    return sorted(range(1, length), key=lambda o: -min(o, length - o))


def dot_nt(a, b):
    return lax.dot_general(a, b, (((1,), (1,)), ((), ())), preferred_element_type=F32)


def dot_nn(a, b):
    return lax.dot_general(a, b, (((1,), (0,)), ((), ())), preferred_element_type=F32)


def remote(src, dst, send, recv, device):
    return pltpu.make_async_remote_copy(
        src_ref=src, dst_ref=dst, send_sem=send, recv_sem=recv,
        device_id=device, device_id_type=MESH,
    )


def make_kernel(sizes, blocks, tokens, hd, fh):
    ny, nx, nz = sizes
    half = fh // 2
    rows = 2 * half // ny
    rest = half // ny
    cols = hd // nx
    wrows = hd // (nx * ny * 2)
    pieces = nx * ny

    def kernel(
        q_hbm, k_hbm, v_hbm, r_hbm, f_hbm, out_ref,
        kbuf, dbuf, qbuf, vbuf, rbuf, dsrc, fpc, wag,
        a_send, a_land, a_send2, a_land2, a_all,
        b_send, b_land, b_send2, b_land2, b_all,
        wf, wb, pbuf, acts, slopes,
        zall, zfirst, zsend, frecv, fsend, lsem, fpsem, wrecv, wsend,
        a_recv1, a_sem1, a_recv2, a_sem2, a_recv3, a_sem3,
        b_recv1, b_sem1, b_recv2, b_sem2, b_recv3, b_sem3,
    ):
        y, x, c, z = (lax.axis_index(a) for a in ("y", "x", "c", "z"))
        oc = 1 - c

        def at_y(o):
            return lax.rem(y + o, ny)

        def at_x(o):
            return lax.rem(x + o, nx)

        def at_z(o):
            return lax.rem(z + o, nz)

        barrier = pltpu.get_barrier_semaphore()
        greet = [{"z": at_z(o)} for o in range(1, nz)]
        greet += [{"x": at_x(o)} for o in range(1, nx)]
        greet += [{"y": at_y(o)} for o in range(1, ny)]
        greet += [{"c": oc}]

        load_v = pltpu.make_async_copy(v_hbm, vbuf, lsem.at[0])
        load_r = pltpu.make_async_copy(r_hbm, rbuf, lsem.at[1])
        load_f = pltpu.make_async_copy(
            f_hbm.at[0, :, :, pl.ds(pl.multiple_of(c * half, half), half)], fpc.at[c], lsem.at[2]
        )
        load_v.start()
        load_r.start()
        load_f.start()
        for device in greet:
            pl.semaphore_signal(barrier, inc=1, device_id=device, device_id_type=MESH)
        pl.semaphore_wait(barrier, len(greet))

        def head_columns(ref, b, t):
            return ref.at[b, :, pl.ds(pl.multiple_of(t * hd, hd), hd)]

        def z_sem(kind, b):
            return zfirst.at[z] if (kind, b) == (1, 0) else zall.at[kind, b]

        def arrived(ref, sem):
            pltpu.make_async_copy(ref, ref, sem).wait()

        def z_send(kind, b, source, target):
            for o in far_first(nz):
                t = at_z(o)
                remote(source(t), target, zsend.at[kind, b], z_sem(kind, b), {"z": t}).start()
            pltpu.make_async_copy(source(z), target, z_sem(kind, b)).start()

        def send_keys(b):
            z_send(0, b, lambda t: head_columns(k_hbm, b, t), kbuf.at[b, c, z])

        def send_grads(b):
            z_send(1, b, lambda t: dsrc.at[b, t], dbuf.at[b, c, z])

        def send_queries(b):
            z_send(2, b, lambda t: head_columns(q_hbm, b, t), qbuf.at[b, z])

        def scale_values(b):
            rate = rbuf[b].astype(F32).T
            for h in range(nz):
                dsrc[b, h] = (
                    -(rate[:, h : h + 1] * vbuf[b, :, h * hd : (h + 1) * hd].astype(F32))
                ).astype(BF16)

        send_keys(0)
        f_copy = remote(
            f_hbm.at[0, :, :, pl.ds(pl.multiple_of(oc * half, half), half)],
            fpc.at[c], fpsem.at[0], fpsem.at[1], {"c": oc},
        )
        f_copy.start()

        def slot(cc, xx, yy):
            return (cc * nx + xx) * ny + yy

        def across_y(o):
            return {"y": at_y(o)}

        def across_x(o):
            return {"x": at_x(o)}

        def slot_y(cc, oy, ox):
            return slot(cc, at_x(ox), at_y(oy))

        def slot_x(cc, ox, oy):
            return slot(cc, at_x(ox), at_y(oy))

        class Gather:
            def __init__(self, buf, send, recv, n1, at1, peer1, n2, peer2, place):
                self.buf, self.send, self.recv, self.place = buf, send, recv, place
                self.n1, self.at1, self.peer1, self.n2, self.peer2 = n1, at1, peer1, n2, peer2
                self.own = place(c, 0, 0)

            def give(self, s, device, sem):
                remote(self.buf.at[s], self.buf.at[s], self.send, self.recv.at[sem], device).start()

            def start1(self):
                for o in far_first(self.n1):
                    self.give(self.own, self.peer1(o), self.at1(0))

            def spread(self, s, o):
                for o2 in far_first(self.n2):
                    self.give(s, self.peer2(o2), self.n1 + self.at1(o))
                self.give(s, {"c": oc}, 2 * self.n1)

            def start2(self):
                self.spread(self.own, 0)

            def relay1(self):
                for o in reversed(far_first(self.n1)):
                    s = self.place(c, o, 0)
                    arrived(self.buf.at[s], self.recv.at[self.at1(o)])
                    self.spread(s, o)
                    yield

            def relay2(self):
                for o in [0] + list(reversed(far_first(self.n1))):
                    arrived(self.buf.at[0 : self.n2 - 1], self.recv.at[self.n1 + self.at1(o)])
                    for o2 in far_first(self.n2):
                        self.give(self.place(c, o, o2), {"c": oc}, 2 * self.n1)
                    yield

            def end(self):
                arrived(self.buf.at[pl.ds(oc * pieces, pieces)], self.recv.at[2 * self.n1])

        def run(*pairs):
            live = list(pairs)
            while live:
                for pair in list(live):
                    steps, many = pair
                    for _ in range(many):
                        try:
                            next(steps)
                        except StopIteration:
                            live.remove(pair)
                            break

        load_f.wait()
        f_copy.wait_recv()
        wag[slot(c, x, y)] = jnp.concatenate([fpc[0], fpc[1]], axis=1).astype(BF16)
        weights_gather = Gather(wag, wsend, wrecv, ny, at_y, across_y, nx, across_x, slot_y)
        weights_gather.start1()
        weights_gather.start2()
        load_v.wait()
        load_r.wait()
        scale_values(0)
        send_grads(0)
        run((weights_gather.relay1(), 1))
        run((weights_gather.relay2(), 1))

        def forward(b, kind, buf):
            if (kind, b) == (1, 0):
                for o in far_first(nz) + [0]:
                    zs = lax.rem(z - o + nz, nz)
                    mine = buf.at[b, c, zs]
                    arrived(mine, zfirst.at[zs])
                    remote(mine, mine, fsend.at[b, kind], frecv.at[b, kind], {"c": oc}).start()
            else:
                mine = buf.at[b, c]
                arrived(mine, zall.at[kind, b])
                remote(mine, mine, fsend.at[b, kind], frecv.at[b, kind], {"c": oc}).start()

        def forwarded(b, kind, buf):
            arrived(buf.at[b, oc], frecv.at[b, kind])

        count = nz * tokens

        def keys_part(b, cc):
            keys = kbuf[b, cc].reshape(count, hd)
            gate_up = dot_nt(keys, jnp.concatenate([wb[0, c], wb[1, c]], axis=0))
            gate, up = gate_up[:, :half], gate_up[:, half:]
            sig = jax.nn.sigmoid(gate)
            act = gate * sig
            acts[cc] = act
            slopes[cc] = up * (sig * (1.0 + gate * (1.0 - sig)))
            pbuf[cc, :, 2 * half : 3 * half] = (act * up).astype(BF16)

        def grads_part(b, cc):
            hidden_grad = dot_nt(dbuf[b, cc].reshape(count, hd), wb[2, c])
            pbuf[cc, :, 0:half] = (hidden_grad * slopes[cc]).astype(BF16)
            pbuf[cc, :, half : 2 * half] = (hidden_grad * acts[cc]).astype(BF16)

        forward(0, 0, kbuf)
        weights_gather.end()
        for m in range(3):
            for cc in range(2):
                part = jnp.concatenate(
                    [wag[slot(cc, xx, yy), m] for yy in range(ny) for xx in range(nx)], axis=0
                )
                turned = part.T
                wb[m, cc] = turned
                wf[m, cc] = turned.astype(F32)
        keys_part(0, c)
        forwarded(0, 0, kbuf)
        keys_part(0, oc)
        forward(0, 1, dbuf)

        def gradients(b):
            keys = kbuf[b].reshape(2 * count, hd)
            out_grad = dbuf[b].reshape(2 * count, hd)
            turned = pbuf[...].reshape(2 * count, 3 * half).T
            third = dot_nn(turned[2 * half :], out_grad)
            for xx in range(nx):
                b_send[b, :, xx] = third[:, xx * cols : (xx + 1) * cols].astype(BF16).reshape(ny, rest, cols)
            both = dot_nn(turned[: 2 * half], keys)
            for xx in range(nx):
                a_send[b, xx] = both[:, xx * cols : (xx + 1) * cols].astype(BF16).reshape(ny, rows, cols)

        class Reduce:
            def __init__(self, b, bufs, sems, n1, at1, name1, me1, n2, at2, name2):
                self.send, self.land, self.send2, self.land2 = (r.at[b] for r in bufs)
                self.recv1, self.sem1, self.recv2, self.sem2 = (r.at[b] for r in sems)
                self.n1, self.at1, self.name1, self.me1 = n1, at1, name1, me1
                self.n2, self.at2, self.name2 = n2, at2, name2

            def start(self):
                for o in far_first(self.n2) + [0]:
                    end = self.at2(o)
                    for o1 in far_first(self.n1):
                        t = self.at1(o1)
                        remote(
                            self.send.at[t, end], self.land.at[o1 - 1, end],
                            self.sem1, self.recv1.at[end], {self.name1: t},
                        ).start()

            def steps(self, result, where):
                total = None
                for o in far_first(self.n2) + [0]:
                    end = self.at2(o)
                    total = self.send[self.me1, end].astype(F32)
                    arrived(self.land.at[:, end], self.recv1.at[end])
                    for o1 in range(1, self.n1):
                        total = total + self.land[o1 - 1, end].astype(F32)
                    if o:
                        self.send2[o - 1] = total.astype(BF16)
                        remote(
                            self.send2.at[o - 1], self.land2.at[o - 1],
                            self.sem2, self.recv2, {self.name2: end},
                        ).start()
                    yield
                arrived(self.land2, self.recv2)
                for o in far_first(self.n2):
                    total = total + self.land2[o - 1].astype(F32)
                result[where] = total.astype(BF16)

        def sums(b):
            return (
                Reduce(
                    b, (a_send, a_land, a_send2, a_land2), (a_recv1, a_sem1, a_recv2, a_sem2),
                    nx, at_x, "x", x, ny, at_y, "y",
                ),
                Reduce(
                    b, (b_send, b_land, b_send2, b_land2), (b_recv1, b_sem1, b_recv2, b_sem2),
                    ny, at_y, "y", y, nx, at_x, "x",
                ),
            )

        def start_reduce(b):
            for part in reversed(sums(b)):
                part.start()

        def finish_reduce(b):
            first, second = sums(b)
            own = slot(c, x, y)
            run((first.steps(a_all.at[b], own), 2), (second.steps(b_all.at[b], own), 1))
            ga = Gather(a_all.at[b], a_sem3.at[b], a_recv3.at[b], ny, at_y, across_y, nx, across_x, slot_y)
            gb = Gather(b_all.at[b], b_sem3.at[b], b_recv3.at[b], nx, at_x, across_x, ny, across_y, slot_x)
            ga.start1()
            gb.start1()
            ga.start2()
            gb.start2()
            run((gb.relay1(), 1))
            run((ga.relay1(), 1))
            run((ga.relay2(), 1), (gb.relay2(), 1))
            ga.end()
            gb.end()

        def update(b):
            lows = []
            for m in range(3):
                halves = []
                for cc in range(2):
                    parts = []
                    for xx in range(nx):
                        first_slot = slot(cc, xx, 0)
                        if m < 2:
                            whole = a_all[b, first_slot : first_slot + ny].reshape(2 * half, cols)
                            parts.append(whole[m * half : (m + 1) * half])
                        else:
                            parts.append(b_all[b, first_slot : first_slot + ny].reshape(half, cols))
                    halves.append(jnp.concatenate(parts, axis=1))
                lows.append(jnp.concatenate(halves, axis=0))
            grams = [dot_nt(low, low) for low in lows]
            inverses = []
            for low in lows:
                full = low.astype(F32)
                inverses.append(1.0 / (jnp.sqrt(jnp.sum(full * full, keepdims=True)) + EPSILON))
            grams = [g * (i * i) for g, i in zip(grams, inverses)]
            polys = [COEF_B * g + COEF_C * dot_nn(g.astype(BF16), g.astype(BF16)) for g in grams]
            firsts = [
                (COEF_A * low.astype(F32) + dot_nn(p.astype(BF16), low)) * i
                for low, p, i in zip(lows, polys, inverses)
            ]
            first_lows = [f.astype(BF16) for f in firsts]
            grams = [dot_nt(f, f) for f in first_lows]
            polys = [COEF_B * g + COEF_C * dot_nn(g.astype(BF16), g.astype(BF16)) for g in grams]
            for m in range(3):
                second = COEF_A * firsts[m] + dot_nn(polys[m].astype(BF16), first_lows[m])
                fresh = wf[m].reshape(fh, hd) - LEARNING_STEP * second
                wf[m] = fresh.reshape(2, half, hd)
                wb[m] = fresh.astype(BF16).reshape(2, half, hd)

        def answer(b):
            queries = qbuf[b].reshape(count, hd)
            gate = dot_nt(queries, wb[0].reshape(fh, hd))
            up = dot_nt(queries, wb[1].reshape(fh, hd))
            hidden = (gate * jax.nn.sigmoid(gate) * up).astype(BF16)
            out_ref[b] = dot_nn(hidden, wb[2].reshape(fh, hd)).astype(BF16)

        for b in range(1, blocks):
            send_keys(b)

        for b in range(blocks):
            grads_part(b, c)
            forwarded(b, 1, dbuf)
            grads_part(b, oc)
            gradients(b)
            start_reduce(b)
            if b == 0:
                for later in range(1, blocks):
                    scale_values(later)
                    send_grads(later)
                for each in range(blocks):
                    send_queries(each)
            else:
                arrived(qbuf.at[b - 1], zall.at[2, b - 1])
                answer(b - 1)
            finish_reduce(b)
            if b + 1 < blocks:
                forward(b + 1, 0, kbuf)
                forward(b + 1, 1, dbuf)
            update(b)
            if b + 1 < blocks:
                keys_part(b + 1, c)
                forwarded(b + 1, 0, kbuf)
                keys_part(b + 1, oc)
        last = blocks - 1
        arrived(qbuf.at[last], zall.at[2, last])
        answer(last)

        def sent(ref, sem):
            pltpu.make_async_copy(ref, ref, sem).wait()

        for b in range(blocks):
            for kind in range(3):
                sent(qbuf.at[0, 0 : nz - 1], zsend.at[kind, b])
            for kind in range(2):
                sent(kbuf.at[b, 0], fsend.at[b, kind])
            sent(a_send.at[b, 0 : nx - 1], a_sem1.at[b])
            sent(b_send.at[b, 0 : ny - 1], b_sem1.at[b])
            sent(a_send2.at[b], a_sem2.at[b])
            sent(b_send2.at[b], b_sem2.at[b])
            sent(a_all.at[b, 0 : 2 * pieces - 1], a_sem3.at[b])
            sent(b_all.at[b, 0 : 2 * pieces - 1], b_sem3.at[b])
        sent(wag.at[0 : 2 * pieces - 1], wsend)
        f_copy.wait_send()

    dma = pltpu.SemaphoreType.DMA
    scratch = [
        pltpu.VMEM((blocks, 2, nz, tokens, hd), BF16),
        pltpu.VMEM((blocks, 2, nz, tokens, hd), BF16),
        pltpu.VMEM((blocks, nz, tokens, hd), BF16),
        pltpu.VMEM((blocks, tokens, nz * hd), BF16),
        pltpu.VMEM((blocks, nz, tokens), BF16),
        pltpu.VMEM((blocks, nz, tokens, hd), BF16),
        pltpu.VMEM((2, 3, wrows, half), F32),
        pltpu.VMEM((2 * pieces, 3, 2 * wrows, half), BF16),
        pltpu.VMEM((blocks, nx, ny, rows, cols), BF16),
        pltpu.VMEM((blocks, nx - 1, ny, rows, cols), BF16),
        pltpu.VMEM((blocks, ny - 1, rows, cols), BF16),
        pltpu.VMEM((blocks, ny - 1, rows, cols), BF16),
        pltpu.VMEM((blocks, 2 * pieces, rows, cols), BF16),
        pltpu.VMEM((blocks, ny, nx, rest, cols), BF16),
        pltpu.VMEM((blocks, ny - 1, nx, rest, cols), BF16),
        pltpu.VMEM((blocks, nx - 1, rest, cols), BF16),
        pltpu.VMEM((blocks, nx - 1, rest, cols), BF16),
        pltpu.VMEM((blocks, 2 * pieces, rest, cols), BF16),
        pltpu.VMEM((3, 2, half, hd), F32),
        pltpu.VMEM((3, 2, half, hd), BF16),
        pltpu.VMEM((2, nz * tokens, 3 * half), BF16),
        pltpu.VMEM((2, nz * tokens, half), F32),
        pltpu.VMEM((2, nz * tokens, half), F32),
        dma((3, blocks)),
        dma((nz,)),
        dma((3, blocks)),
        dma((blocks, 2)),
        dma((blocks, 2)),
        dma((3,)),
        dma((2,)),
        dma((2 * ny + 1,)),
        dma(()),
        dma((blocks, ny)),
        dma((blocks,)),
        dma((blocks,)),
        dma((blocks,)),
        dma((blocks, 2 * ny + 1)),
        dma((blocks,)),
        dma((blocks, nx)),
        dma((blocks,)),
        dma((blocks,)),
        dma((blocks,)),
        dma((blocks, 2 * nx + 1)),
        dma((blocks,)),
    ]
    return kernel, scratch


def build(mesh):
    ny, nx, _, nz = (mesh.shape[a] for a in ("y", "x", "c", "z"))

    def local(queries, keys, values, rates, fast_init):
        blocks, tokens, width = queries.shape
        hd = width // nz
        fh = fast_init.shape[3]
        kernel, scratch = make_kernel((ny, nx, nz), blocks, tokens, hd, fh)
        return pl.pallas_call(
            kernel,
            out_shape=pltpu.VMEM((blocks, nz * tokens, hd), BF16),
            in_specs=[pl.BlockSpec(memory_space=pl.ANY)] * 5,
            out_specs=pl.BlockSpec(memory_space=pltpu.VMEM),
            scratch_shapes=scratch,
            compiler_params=pltpu.CompilerParams(
                collective_id=0, has_side_effects=True, vmem_limit_bytes=60 * 1024 * 1024
            ),
        )(queries, keys, values, jnp.swapaxes(rates, 1, 2), fast_init)

    tokens_at = ("y", "x", "c", "z")
    in_specs = (
        P(None, tokens_at, None),
        P(None, tokens_at, None),
        P(None, tokens_at, None),
        P(None, tokens_at, None),
        P("z", None, ("y", "x", "c"), None),
    )
    out_specs = P(None, ("y", "x", "c"), "z")
    return jax.shard_map(local, mesh=mesh, in_specs=in_specs, out_specs=out_specs, check_vma=False)


def solution(mesh):
    seq, heads = mesh.shape["seq"], mesh.shape["head"]
    return build(Mesh(mesh.devices.reshape(seq // 8, 4, 2, heads), ("y", "x", "c", "z")))
```

```python
import jax
import jax.numpy as jnp
from jax import lax
from jax.experimental import pallas as pl
from jax.experimental.pallas import tpu as pltpu
from jax.sharding import Mesh
from jax.sharding import PartitionSpec as P

EPSILON = 1e-06
COEF_A = 3.4445
COEF_B = -4.775
COEF_C = 2.0315
LEARNING_STEP = 0.5
MESH = pl.DeviceIdType.MESH
BF16 = jnp.bfloat16
F32 = jnp.float32


def far_first(length):
    return sorted(range(1, length), key=lambda o: -min(o, length - o))


def dot_nt(a, b):
    return lax.dot_general(a, b, (((1,), (1,)), ((), ())), preferred_element_type=F32)


def dot_nn(a, b):
    return lax.dot_general(a, b, (((1,), (0,)), ((), ())), preferred_element_type=F32)


def remote(src, dst, send, recv, device):
    return pltpu.make_async_remote_copy(
        src_ref=src, dst_ref=dst, send_sem=send, recv_sem=recv,
        device_id=device, device_id_type=MESH,
    )


def make_kernel(sizes, blocks, tokens, hd, fh):
    ny, nx, nz = sizes
    half = fh // 2
    rows = 2 * half // ny
    rest = half // ny
    cols = hd // nx
    wrows = hd // (nx * ny * 2)
    pieces = nx * ny

    def kernel(
        q_hbm, k_hbm, v_hbm, r_hbm, f_hbm, out_ref,
        kbuf, dbuf, qbuf, vbuf, rbuf, dsrc, fpc, wag,
        a_send, a_land, a_send2, a_land2, a_all,
        b_send, b_land, b_send2, b_land2, b_all,
        wf, wb, pbuf, acts, slopes,
        zall, zfirst, zsend, frecv, fsend, lsem, fpsem, wrecv, wsend,
        a_recv1, a_sem1, a_recv2, a_sem2, a_recv3, a_sem3,
        b_recv1, b_sem1, b_recv2, b_sem2, b_recv3, b_sem3,
    ):
        y, x, c, z = (lax.axis_index(a) for a in ("y", "x", "c", "z"))
        oc = 1 - c

        def at_y(o):
            return lax.rem(y + o, ny)

        def at_x(o):
            return lax.rem(x + o, nx)

        def at_z(o):
            return lax.rem(z + o, nz)

        barrier = pltpu.get_barrier_semaphore()
        greet = [{"z": at_z(o)} for o in range(1, nz)]
        greet += [{"x": at_x(o)} for o in range(1, nx)]
        greet += [{"y": at_y(o)} for o in range(1, ny)]
        greet += [{"c": oc}]

        load_v = pltpu.make_async_copy(v_hbm, vbuf, lsem.at[0])
        load_r = pltpu.make_async_copy(r_hbm, rbuf, lsem.at[1])
        load_f = pltpu.make_async_copy(
            f_hbm.at[0, :, :, pl.ds(pl.multiple_of(c * half, half), half)], fpc.at[c], lsem.at[2]
        )
        load_v.start()
        load_r.start()
        load_f.start()
        for device in greet:
            pl.semaphore_signal(barrier, inc=1, device_id=device, device_id_type=MESH)
        pl.semaphore_wait(barrier, len(greet))

        def head_columns(ref, b, t):
            return ref.at[b, :, pl.ds(pl.multiple_of(t * hd, hd), hd)]

        def z_sem(kind, b):
            return zfirst.at[z] if (kind, b) == (1, 0) else zall.at[kind, b]

        def arrived(ref, sem):
            pltpu.make_async_copy(ref, ref, sem).wait()

        def z_send(kind, b, source, target):
            for o in far_first(nz):
                t = at_z(o)
                remote(source(t), target, zsend.at[kind, b], z_sem(kind, b), {"z": t}).start()
            pltpu.make_async_copy(source(z), target, z_sem(kind, b)).start()

        def send_keys(b):
            z_send(0, b, lambda t: head_columns(k_hbm, b, t), kbuf.at[b, c, z])

        def send_grads(b):
            z_send(1, b, lambda t: dsrc.at[b, t], dbuf.at[b, c, z])

        def send_queries(b):
            z_send(2, b, lambda t: head_columns(q_hbm, b, t), qbuf.at[b, z])

        def scale_values(b):
            rate = rbuf[b].astype(F32).T
            for h in range(nz):
                dsrc[b, h] = (
                    -(rate[:, h : h + 1] * vbuf[b, :, h * hd : (h + 1) * hd].astype(F32))
                ).astype(BF16)

        send_keys(0)
        f_copy = remote(
            f_hbm.at[0, :, :, pl.ds(pl.multiple_of(oc * half, half), half)],
            fpc.at[c], fpsem.at[0], fpsem.at[1], {"c": oc},
        )
        f_copy.start()

        def slot(cc, xx, yy):
            return (cc * nx + xx) * ny + yy

        def across_y(o):
            return {"y": at_y(o)}

        def across_x(o):
            return {"x": at_x(o)}

        def slot_y(cc, oy, ox):
            return slot(cc, at_x(ox), at_y(oy))

        def slot_x(cc, ox, oy):
            return slot(cc, at_x(ox), at_y(oy))

        class Gather:
            def __init__(self, buf, send, recv, n1, at1, peer1, n2, peer2, place):
                self.buf, self.send, self.recv, self.place = buf, send, recv, place
                self.n1, self.at1, self.peer1, self.n2, self.peer2 = n1, at1, peer1, n2, peer2
                self.own = place(c, 0, 0)

            def give(self, s, device, sem):
                remote(self.buf.at[s], self.buf.at[s], self.send, self.recv.at[sem], device).start()

            def start1(self):
                for o in far_first(self.n1):
                    self.give(self.own, self.peer1(o), self.at1(0))

            def spread(self, s, o):
                for o2 in far_first(self.n2):
                    self.give(s, self.peer2(o2), self.n1 + self.at1(o))
                self.give(s, {"c": oc}, 2 * self.n1)

            def start2(self):
                self.spread(self.own, 0)

            def relay1(self):
                for o in reversed(far_first(self.n1)):
                    s = self.place(c, o, 0)
                    arrived(self.buf.at[s], self.recv.at[self.at1(o)])
                    self.spread(s, o)
                    yield

            def relay2(self):
                for o in [0] + list(reversed(far_first(self.n1))):
                    arrived(self.buf.at[0 : self.n2 - 1], self.recv.at[self.n1 + self.at1(o)])
                    for o2 in far_first(self.n2):
                        self.give(self.place(c, o, o2), {"c": oc}, 2 * self.n1)
                    yield

            def end(self):
                arrived(self.buf.at[pl.ds(oc * pieces, pieces)], self.recv.at[2 * self.n1])

        def run(*pairs):
            live = list(pairs)
            while live:
                for pair in list(live):
                    steps, many = pair
                    for _ in range(many):
                        try:
                            next(steps)
                        except StopIteration:
                            live.remove(pair)
                            break

        load_f.wait()
        f_copy.wait_recv()
        wag[slot(c, x, y)] = jnp.concatenate([fpc[0], fpc[1]], axis=1).astype(BF16)
        weights_gather = Gather(wag, wsend, wrecv, ny, at_y, across_y, nx, across_x, slot_y)
        weights_gather.start1()
        weights_gather.start2()
        load_v.wait()
        load_r.wait()
        scale_values(0)
        send_grads(0)
        run((weights_gather.relay1(), 1))
        run((weights_gather.relay2(), 1))

        def forward(b, kind, buf):
            if (kind, b) == (1, 0):
                for o in far_first(nz) + [0]:
                    zs = lax.rem(z - o + nz, nz)
                    mine = buf.at[b, c, zs]
                    arrived(mine, zfirst.at[zs])
                    remote(mine, mine, fsend.at[b, kind], frecv.at[b, kind], {"c": oc}).start()
            else:
                mine = buf.at[b, c]
                arrived(mine, zall.at[kind, b])
                remote(mine, mine, fsend.at[b, kind], frecv.at[b, kind], {"c": oc}).start()

        def forwarded(b, kind, buf):
            arrived(buf.at[b, oc], frecv.at[b, kind])

        count = nz * tokens

        def keys_part(b, cc):
            keys = kbuf[b, cc].reshape(count, hd)
            gate_up = dot_nt(keys, jnp.concatenate([wb[0, c], wb[1, c]], axis=0))
            gate, up = gate_up[:, :half], gate_up[:, half:]
            sig = jax.nn.sigmoid(gate)
            act = gate * sig
            acts[cc] = act
            slopes[cc] = up * (sig * (1.0 + gate * (1.0 - sig)))
            pbuf[cc, :, 2 * half : 3 * half] = (act * up).astype(BF16)

        def grads_part(b, cc):
            hidden_grad = dot_nt(dbuf[b, cc].reshape(count, hd), wb[2, c])
            pbuf[cc, :, 0:half] = (hidden_grad * slopes[cc]).astype(BF16)
            pbuf[cc, :, half : 2 * half] = (hidden_grad * acts[cc]).astype(BF16)

        forward(0, 0, kbuf)
        weights_gather.end()
        for m in range(3):
            for cc in range(2):
                part = jnp.concatenate(
                    [wag[slot(cc, xx, yy), m] for yy in range(ny) for xx in range(nx)], axis=0
                )
                turned = part.T
                wb[m, cc] = turned
                wf[m, cc] = turned.astype(F32)
        keys_part(0, c)
        forwarded(0, 0, kbuf)
        keys_part(0, oc)
        forward(0, 1, dbuf)

        def gradients(b):
            keys = kbuf[b].reshape(2 * count, hd)
            out_grad = dbuf[b].reshape(2 * count, hd)
            turned = pbuf[...].reshape(2 * count, 3 * half).T
            third = dot_nn(turned[2 * half :], out_grad)
            for xx in range(nx):
                b_send[b, :, xx] = third[:, xx * cols : (xx + 1) * cols].astype(BF16).reshape(ny, rest, cols)
            both = dot_nn(turned[: 2 * half], keys)
            for xx in range(nx):
                a_send[b, xx] = both[:, xx * cols : (xx + 1) * cols].astype(BF16).reshape(ny, rows, cols)

        class Reduce:
            def __init__(self, b, bufs, sems, n1, at1, name1, me1, n2, at2, name2):
                self.send, self.land, self.send2, self.land2 = (r.at[b] for r in bufs)
                self.recv1, self.sem1, self.recv2, self.sem2 = (r.at[b] for r in sems)
                self.n1, self.at1, self.name1, self.me1 = n1, at1, name1, me1
                self.n2, self.at2, self.name2 = n2, at2, name2

            def start(self):
                for o in far_first(self.n2) + [0]:
                    end = self.at2(o)
                    for o1 in far_first(self.n1):
                        t = self.at1(o1)
                        remote(
                            self.send.at[t, end], self.land.at[o1 - 1, end],
                            self.sem1, self.recv1.at[end], {self.name1: t},
                        ).start()

            def steps(self, result, where):
                total = None
                for o in far_first(self.n2) + [0]:
                    end = self.at2(o)
                    total = self.send[self.me1, end].astype(F32)
                    arrived(self.land.at[:, end], self.recv1.at[end])
                    for o1 in range(1, self.n1):
                        total = total + self.land[o1 - 1, end].astype(F32)
                    if o:
                        self.send2[o - 1] = total.astype(BF16)
                        remote(
                            self.send2.at[o - 1], self.land2.at[o - 1],
                            self.sem2, self.recv2, {self.name2: end},
                        ).start()
                    yield
                arrived(self.land2, self.recv2)
                for o in far_first(self.n2):
                    total = total + self.land2[o - 1].astype(F32)
                result[where] = total.astype(BF16)

        def sums(b):
            return (
                Reduce(
                    b, (a_send, a_land, a_send2, a_land2), (a_recv1, a_sem1, a_recv2, a_sem2),
                    nx, at_x, "x", x, ny, at_y, "y",
                ),
                Reduce(
                    b, (b_send, b_land, b_send2, b_land2), (b_recv1, b_sem1, b_recv2, b_sem2),
                    ny, at_y, "y", y, nx, at_x, "x",
                ),
            )

        def start_reduce(b):
            for part in reversed(sums(b)):
                part.start()

        def finish_reduce(b):
            first, second = sums(b)
            own = slot(c, x, y)
            run((first.steps(a_all.at[b], own), 2), (second.steps(b_all.at[b], own), 1))
            ga = Gather(a_all.at[b], a_sem3.at[b], a_recv3.at[b], ny, at_y, across_y, nx, across_x, slot_y)
            gb = Gather(b_all.at[b], b_sem3.at[b], b_recv3.at[b], nx, at_x, across_x, ny, across_y, slot_x)
            ga.start1()
            gb.start1()
            ga.start2()
            gb.start2()
            run((gb.relay1(), 1))
            run((ga.relay1(), 1))
            run((gb.relay2(), 1))
            run((ga.relay2(), 1))
            ga.end()
            gb.end()

        def update(b):
            lows = []
            for m in range(3):
                halves = []
                for cc in range(2):
                    parts = []
                    for xx in range(nx):
                        first_slot = slot(cc, xx, 0)
                        if m < 2:
                            whole = a_all[b, first_slot : first_slot + ny].reshape(2 * half, cols)
                            parts.append(whole[m * half : (m + 1) * half])
                        else:
                            parts.append(b_all[b, first_slot : first_slot + ny].reshape(half, cols))
                    halves.append(jnp.concatenate(parts, axis=1))
                lows.append(jnp.concatenate(halves, axis=0))
            grams = [dot_nt(low, low) for low in lows]
            inverses = []
            for low in lows:
                full = low.astype(F32)
                inverses.append(1.0 / (jnp.sqrt(jnp.sum(full * full, keepdims=True)) + EPSILON))
            grams = [g * (i * i) for g, i in zip(grams, inverses)]
            polys = [COEF_B * g + COEF_C * dot_nn(g.astype(BF16), g.astype(BF16)) for g in grams]
            firsts = [
                (COEF_A * low.astype(F32) + dot_nn(p.astype(BF16), low)) * i
                for low, p, i in zip(lows, polys, inverses)
            ]
            first_lows = [f.astype(BF16) for f in firsts]
            grams = [dot_nt(f, f) for f in first_lows]
            polys = [COEF_B * g + COEF_C * dot_nn(g.astype(BF16), g.astype(BF16)) for g in grams]
            for m in range(3):
                second = COEF_A * firsts[m] + dot_nn(polys[m].astype(BF16), first_lows[m])
                fresh = wf[m].reshape(fh, hd) - LEARNING_STEP * second
                wf[m] = fresh.reshape(2, half, hd)
                wb[m] = fresh.astype(BF16).reshape(2, half, hd)

        def answer(b):
            queries = qbuf[b].reshape(count, hd)
            gate = dot_nt(queries, wb[0].reshape(fh, hd))
            up = dot_nt(queries, wb[1].reshape(fh, hd))
            hidden = (gate * jax.nn.sigmoid(gate) * up).astype(BF16)
            out_ref[b] = dot_nn(hidden, wb[2].reshape(fh, hd)).astype(BF16)

        for b in range(1, blocks):
            send_keys(b)

        for b in range(blocks):
            grads_part(b, c)
            forwarded(b, 1, dbuf)
            grads_part(b, oc)
            gradients(b)
            start_reduce(b)
            if b == 0:
                for later in range(1, blocks):
                    scale_values(later)
                    send_grads(later)
                for each in range(blocks):
                    send_queries(each)
            else:
                arrived(qbuf.at[b - 1], zall.at[2, b - 1])
                answer(b - 1)
            finish_reduce(b)
            if b + 1 < blocks:
                forward(b + 1, 0, kbuf)
                forward(b + 1, 1, dbuf)
            update(b)
            if b + 1 < blocks:
                keys_part(b + 1, c)
                forwarded(b + 1, 0, kbuf)
                keys_part(b + 1, oc)
        last = blocks - 1
        arrived(qbuf.at[last], zall.at[2, last])
        answer(last)

        def sent(ref, sem):
            pltpu.make_async_copy(ref, ref, sem).wait()

        for b in range(blocks):
            for kind in range(3):
                sent(qbuf.at[0, 0 : nz - 1], zsend.at[kind, b])
            for kind in range(2):
                sent(kbuf.at[b, 0], fsend.at[b, kind])
            sent(a_send.at[b, 0 : nx - 1], a_sem1.at[b])
            sent(b_send.at[b, 0 : ny - 1], b_sem1.at[b])
            sent(a_send2.at[b], a_sem2.at[b])
            sent(b_send2.at[b], b_sem2.at[b])
            sent(a_all.at[b, 0 : 2 * pieces - 1], a_sem3.at[b])
            sent(b_all.at[b, 0 : 2 * pieces - 1], b_sem3.at[b])
        sent(wag.at[0 : 2 * pieces - 1], wsend)
        f_copy.wait_send()

    dma = pltpu.SemaphoreType.DMA
    scratch = [
        pltpu.VMEM((blocks, 2, nz, tokens, hd), BF16),
        pltpu.VMEM((blocks, 2, nz, tokens, hd), BF16),
        pltpu.VMEM((blocks, nz, tokens, hd), BF16),
        pltpu.VMEM((blocks, tokens, nz * hd), BF16),
        pltpu.VMEM((blocks, nz, tokens), BF16),
        pltpu.VMEM((blocks, nz, tokens, hd), BF16),
        pltpu.VMEM((2, 3, wrows, half), F32),
        pltpu.VMEM((2 * pieces, 3, 2 * wrows, half), BF16),
        pltpu.VMEM((blocks, nx, ny, rows, cols), BF16),
        pltpu.VMEM((blocks, nx - 1, ny, rows, cols), BF16),
        pltpu.VMEM((blocks, ny - 1, rows, cols), BF16),
        pltpu.VMEM((blocks, ny - 1, rows, cols), BF16),
        pltpu.VMEM((blocks, 2 * pieces, rows, cols), BF16),
        pltpu.VMEM((blocks, ny, nx, rest, cols), BF16),
        pltpu.VMEM((blocks, ny - 1, nx, rest, cols), BF16),
        pltpu.VMEM((blocks, nx - 1, rest, cols), BF16),
        pltpu.VMEM((blocks, nx - 1, rest, cols), BF16),
        pltpu.VMEM((blocks, 2 * pieces, rest, cols), BF16),
        pltpu.VMEM((3, 2, half, hd), F32),
        pltpu.VMEM((3, 2, half, hd), BF16),
        pltpu.VMEM((2, nz * tokens, 3 * half), BF16),
        pltpu.VMEM((2, nz * tokens, half), F32),
        pltpu.VMEM((2, nz * tokens, half), F32),
        dma((3, blocks)),
        dma((nz,)),
        dma((3, blocks)),
        dma((blocks, 2)),
        dma((blocks, 2)),
        dma((3,)),
        dma((2,)),
        dma((2 * ny + 1,)),
        dma(()),
        dma((blocks, ny)),
        dma((blocks,)),
        dma((blocks,)),
        dma((blocks,)),
        dma((blocks, 2 * ny + 1)),
        dma((blocks,)),
        dma((blocks, nx)),
        dma((blocks,)),
        dma((blocks,)),
        dma((blocks,)),
        dma((blocks, 2 * nx + 1)),
        dma((blocks,)),
    ]
    return kernel, scratch


def build(mesh):
    ny, nx, _, nz = (mesh.shape[a] for a in ("y", "x", "c", "z"))

    def local(queries, keys, values, rates, fast_init):
        blocks, tokens, width = queries.shape
        hd = width // nz
        fh = fast_init.shape[3]
        kernel, scratch = make_kernel((ny, nx, nz), blocks, tokens, hd, fh)
        return pl.pallas_call(
            kernel,
            out_shape=pltpu.VMEM((blocks, nz * tokens, hd), BF16),
            in_specs=[pl.BlockSpec(memory_space=pl.ANY)] * 5,
            out_specs=pl.BlockSpec(memory_space=pltpu.VMEM),
            scratch_shapes=scratch,
            compiler_params=pltpu.CompilerParams(
                collective_id=0, has_side_effects=True, vmem_limit_bytes=60 * 1024 * 1024
            ),
        )(queries, keys, values, jnp.swapaxes(rates, 1, 2), fast_init)

    tokens_at = ("y", "x", "c", "z")
    in_specs = (
        P(None, tokens_at, None),
        P(None, tokens_at, None),
        P(None, tokens_at, None),
        P(None, tokens_at, None),
        P("z", None, ("y", "x", "c"), None),
    )
    out_specs = P(None, ("y", "x", "c"), "z")
    return jax.shard_map(local, mesh=mesh, in_specs=in_specs, out_specs=out_specs, check_vma=False)


def solution(mesh):
    seq, heads = mesh.shape["seq"], mesh.shape["head"]
    return build(Mesh(mesh.devices.reshape(seq // 8, 4, 2, heads), ("y", "x", "c", "z")))
```
